128 devices in a mesh: dp: 8 (over y, core), expert: 16 (over x, z).
Axes of the slice: x: 4, y: 4, z: 4, core: 2. Of those that a mesh axis runs over, the one named last changes fastest.
Arguments:
- tokens: bfloat16 [8192, 2048], P(('dp', 'expert')), may hold values from -6 to 6
- grad_out: bfloat16 [8192, 2048], P(('dp', 'expert')), may hold values from -6 to 6
- probs: float32 [8192, 128], P(('dp', 'expert')), may hold values from 0.01 to 1
- expert_ids: int32 [8192, 8], P(('dp', 'expert')), may hold values from 0 to 127, all different within a row; in each aligned block of 64 rows (0 to 63, 64 to 127, ...) at most 8 rows name the same one
- w_gate: bfloat16 [128, 2048, 768], P(('dp', 'expert')), may hold values from -0.125 to 0.125
- w_up: bfloat16 [128, 2048, 768], P(('dp', 'expert')), may hold values from -0.125 to 0.125
- w_down: bfloat16 [128, 768, 2048], P(('dp', 'expert')), may hold values from -0.21875 to 0.21875
Outputs:
- d_tokens: bfloat16 [8192, 2048], P(('dp', 'expert'))
- d_probs: float32 [8192, 128], P(('dp', 'expert'))
- d_gate: bfloat16 [128, 2048, 768], P(('dp', 'expert'))
- d_up: bfloat16 [128, 2048, 768], P(('dp', 'expert'))
- d_down: bfloat16 [128, 768, 2048], P(('dp', 'expert'))
The draws below stay inside these ranges and needn't reach their ends.
Inputs may be any that keep to these rules, and one draw needn't show every extreme that they name: `expert_ids`: each token names 8 different experts. In the 64 tokens of one device no expert is named more than 8 times, and in every draw some expert is named exactly 8 times by the tokens of some device.
All inputs are finite; a program needn't handle non-finite values.
Results may differ from the reference program's by a relative error of at most 0.014.
Values may be sent and summed in bfloat16 or wider, within the bound.
No kernel may reach another device: no remote copies, remote signals or barrier semaphores. Data moves between devices by JAX's collectives and lax.ppermute only.
A program may use at most 128 MiB of HBM per device.

```python
import math
import jax
import jax.numpy as jnp
import numpy as np
from jax import lax

D = 2048
FF = 768
TOPK = 8
TOK_DEV = 64
EXPERTS = 128
TOKENS = 8192
CAP = 8
N_DP = 8
N_EXPERT = 16


def level_of(rng, dims, cuts, smallest, top_value):
    def one(dim, blocks):
        heights = jax.random.uniform(jax.random.fold_in(jax.random.fold_in(rng, 6), dim), (blocks,), jnp.float32, smallest / len(cuts), top_value / len(cuts))
        return jnp.repeat(jnp.exp(heights), dims[dim] // blocks).reshape((-1,) + (1,) * (len(dims) - dim - 1))

    gain = one(*cuts[0])
    for cut in cuts[1:]:
        gain = gain * one(*cut)
    return gain


def deal_out(own_key, own, number, rows, count, top, reach, slope):
    ranking = jax.random.permutation(own_key, count)
    heavy_load, ordinary = load_shares(count, rows * top, reach, slope, True), load_shares(count, rows * top, reach, slope, False)
    places = jnp.arange(count)

    def named(tallies, rotation):
        used = int((tallies > 0).sum())
        fixed = max(1, used // 4)
        moved = fixed + (places - fixed + rotation * (used - fixed)) % max(1, count - fixed)
        return jnp.zeros((count,), jnp.int32).at[ranking[jnp.where(places < fixed, places, moved)]].set(jnp.asarray(tallies, jnp.int32))

    tallies = jnp.where(number % 4 == 0, named(heavy_load, number // 4), named(ordinary, number - number // 4 - 1))
    mixed = jax.random.permutation(jax.random.fold_in(own, 3), count)
    giver, taker = mixed[0:count // 2 * 2:2], mixed[1:count // 2 * 2:2]
    margin = jnp.minimum(tallies[giver] - 1, reach - tallies[taker]) // 2
    margin = jnp.where((giver == ranking[0]) | (taker == ranking[0]) | (tallies[taker] == 0), 0, jnp.maximum(margin, 0))
    moved = jax.random.randint(jax.random.fold_in(own, 4), (count // 2,), 0, 1 << 20) % (margin + 1)
    tallies = tallies.at[giver].add(-moved).at[taker].add(moved)
    labels = jnp.searchsorted(jnp.cumsum(tallies), jnp.arange(rows * top), side="right").astype(jnp.int32)
    listing = labels.reshape(top, rows).T
    listing = listing[jax.random.permutation(jax.random.fold_in(own, 1), rows)]
    rotation = jax.random.randint(jax.random.fold_in(own, 2), (rows, 1), 0, top)
    return jnp.take_along_axis(listing, (jnp.arange(top)[None, :] + rotation) % top, axis=1)


def load_shares(amount, total, bound, skew, full):
    loads = [(1 << 20) // math.isqrt(standing ** skew) + 1 for standing in range(1, amount + 1)]
    largest = bound if full else min(bound, max(-(-total // amount), total * loads[0] // sum(loads)))
    least = 1 if total - largest >= amount - 1 else 0
    holding, surplus = [largest] + [least] * (amount - 1), total - largest - least * (amount - 1)
    while surplus > 0:
        free = [i for i in range(1, amount) if holding[i] < largest] or [i for i in range(1, amount) if holding[i] < bound]
        pool, budget = sum([loads[i] for i in free]), surplus
        for i in free:
            more = min(bound - holding[i], max(1, budget * loads[i] // pool), surplus)
            holding[i] = holding[i] + more
            surplus = surplus - more
    return np.array(holding)


def centred(own_key, dims, spread, most, pieces=(), kind=jnp.bfloat16):
    entries = spread * jax.random.normal(own_key, dims, jnp.float32)
    if pieces:
        entries = entries * level_of(own_key, dims, pieces, -0.22, 0.18)
    return jnp.clip(entries, -most, most).astype(kind)


def setup_inputs(seed: int = 0) -> dict:
    key_of = jax.random.split(jax.random.key(seed), 8)
    tokens = centred(key_of[0], (TOKENS, D), 1.0, 6.0, ((0, 128),))
    grad_out = centred(key_of[1], (TOKENS, D), 1.0, 6.0, ((0, 128),))
    probs = jnp.clip(jnp.exp(math.log(1.0) - 4.6051702 * jax.random.uniform(key_of[2], (TOKENS, EXPERTS), jnp.float32) ** level_of(key_of[2], (TOKENS, EXPERTS), ((0, 128),), -0.2, 0.2)), 0.01, 1.0)
    expert_ids_keys = jax.random.split(jax.random.fold_in(key_of[3], 1), TOKENS // TOK_DEV)
    expert_ids_turns = jax.random.permutation(jax.random.fold_in(key_of[3], 3), TOKENS // TOK_DEV)
    expert_ids = jax.vmap(lambda own, number: deal_out(jax.random.fold_in(key_of[3], 2), own, number, TOK_DEV, EXPERTS, TOPK, CAP, 2))(expert_ids_keys, expert_ids_turns).reshape((TOKENS, TOPK))
    w_gate = centred(key_of[4], (EXPERTS, D, FF), D ** -0.5, 0.125, ((0, 128),))
    w_up = centred(key_of[5], (EXPERTS, D, FF), D ** -0.5, 0.125, ((0, 128),))
    w_down = centred(key_of[6], (EXPERTS, FF, D), FF ** -0.5, 0.21875, ((0, 128),))
    return {"tokens": tokens, "grad_out": grad_out, "probs": probs, "expert_ids": expert_ids, "w_gate": w_gate, "w_up": w_up, "w_down": w_down}


aux_weight = 1.0


def right_dot(left, right):
    return lax.dot_general(left, right, (((1,), (1,)), ((), ())), preferred_element_type=jnp.float32)


def left_dot(left, right):
    return lax.dot_general(left, right, (((0,), (0,)), ((), ())), preferred_element_type=jnp.float32)


def expert_backward(in_tokens, in_grads, in_weights, gate_mat, up_mat, down_mat):
    gate_pre = jnp.dot(in_tokens, gate_mat, preferred_element_type=jnp.float32)
    up_pre = jnp.dot(in_tokens, up_mat, preferred_element_type=jnp.float32)
    sig_gate = jax.nn.sigmoid(gate_pre)
    silu_gate = gate_pre * sig_gate
    hidden = (silu_gate * up_pre).astype(jnp.bfloat16)
    back_hidden = right_dot(in_grads, down_mat)
    route_grad = jnp.sum(hidden.astype(jnp.float32) * back_hidden, axis=1).astype(jnp.bfloat16)
    scale_col = in_weights.astype(jnp.float32)[:, None]
    d_hidden = scale_col * back_hidden
    scaled_grad = (scale_col * in_grads.astype(jnp.float32)).astype(jnp.bfloat16)
    d_down = left_dot(hidden, scaled_grad).astype(jnp.bfloat16)
    d_gate_pre = (d_hidden * up_pre * sig_gate * (1.0 + gate_pre * (1.0 - sig_gate))).astype(jnp.bfloat16)
    d_up_pre = (d_hidden * silu_gate).astype(jnp.bfloat16)
    d_gate = left_dot(in_tokens, d_gate_pre).astype(jnp.bfloat16)
    d_up = left_dot(in_tokens, d_up_pre).astype(jnp.bfloat16)
    row_grad = (right_dot(d_gate_pre, gate_mat) + right_dot(d_up_pre, up_mat)).astype(jnp.bfloat16)
    return row_grad, route_grad, d_gate, d_up, d_down


def reference(tokens, grad_out, probs, expert_ids, w_gate, w_up, w_down):
    row_total = TOKENS * TOPK
    slot_rows = N_DP * N_EXPERT * CAP
    flat_ids = expert_ids.reshape(row_total)
    picked = jnp.take_along_axis(probs, expert_ids, axis=1)
    picked_sum = jnp.sum(picked, axis=1, keepdims=True)
    route_weight = (picked / picked_sum).astype(jnp.bfloat16)
    token_pad = jnp.concatenate([tokens, jnp.zeros((1, D), jnp.bfloat16)], axis=0)
    grad_pad = jnp.concatenate([grad_out, jnp.zeros((1, D), jnp.bfloat16)], axis=0)
    weight_pad = jnp.concatenate([route_weight.reshape(row_total), jnp.zeros((1,), jnp.bfloat16)], axis=0)
    row_numbers = jnp.arange(row_total, dtype=jnp.int32)

    def one_expert(carry, inputs):
        grad_acc, route_acc = carry
        expert_index, gate_mat, up_mat, down_mat = inputs
        chosen = flat_ids == expert_index
        position = jnp.cumsum(chosen.astype(jnp.int32), dtype=jnp.int32) - 1
        target = jnp.where(chosen, position, slot_rows)
        pick_rows = jnp.full((slot_rows,), row_total, jnp.int32).at[target].set(row_numbers, mode="drop")
        pick_tok = jnp.where(pick_rows < row_total, pick_rows // TOPK, TOKENS).astype(jnp.int32)
        outputs = expert_backward(token_pad[pick_tok], grad_pad[pick_tok], weight_pad[pick_rows], gate_mat, up_mat, down_mat)
        grad_acc = grad_acc.at[pick_tok].add(outputs[0].astype(jnp.float32), mode="drop")
        route_acc = route_acc.at[pick_rows].set(outputs[1], mode="drop")
        return (grad_acc, route_acc), (outputs[2], outputs[3], outputs[4])

    start = (jnp.zeros((TOKENS, D), jnp.float32), jnp.zeros((row_total,), jnp.bfloat16))
    expert_numbers = jnp.arange(EXPERTS, dtype=jnp.int32)
    (grad_acc, route_acc), (d_gate, d_up, d_down) = lax.scan(one_expert, start, (expert_numbers, w_gate, w_up, w_down))
    d_tokens = grad_acc.astype(jnp.bfloat16)
    route_grad = route_acc.reshape(TOKENS, TOPK).astype(jnp.float32)
    weight_f = route_weight.astype(jnp.float32)
    d_picked = (route_grad - jnp.sum(route_grad * weight_f, axis=1, keepdims=True)) / picked_sum
    onehot_rows = (expert_ids[:, :, None] == jnp.arange(EXPERTS, dtype=jnp.int32)[None, None, :]).astype(jnp.float32)
    load = jnp.sum(onehot_rows, axis=(0, 1))
    d_probs = jnp.sum(d_picked[:, :, None] * onehot_rows, axis=1) + aux_weight * EXPERTS * load / (TOKENS * TOPK)
    return d_tokens, d_probs, d_gate, d_up, d_down
```

```python
import jax
import jax.numpy as jnp
from jax import lax
from jax.experimental import pallas as pl
from jax.experimental.pallas import tpu as pltpu
from jax.sharding import PartitionSpec as P

aux_weight = 1.0
CAP = 8
LANES = 128
AXES = ("dp", "expert")
f32 = jnp.float32
bf16 = jnp.bfloat16


def iota(shape, dim):
    return lax.broadcasted_iota(jnp.int32, shape, dim)


def nn(left, right):
    return jnp.dot(left, right, preferred_element_type=f32)


def nt(left, right):
    return lax.dot_general(left, right, (((1,), (1,)), ((), ())), preferred_element_type=f32)


def tn(left, right):
    return lax.dot_general(left, right, (((0,), (0,)), ((), ())), preferred_element_type=f32)


def send_kernel(ids_ref, probs_ref, tok_ref, grad_ref, x_ref, pick_ref, w_ref, sum_ref, cnt_ref, rank_s, w_s):
    step = pl.program_id(0)
    rows = x_ref.shape[0]
    toks, experts = probs_ref.shape
    width = tok_ref.shape[1]

    @pl.when(step == 0)
    def _():
        lane = iota((toks, experts), 1)
        member = jnp.zeros((toks, experts), jnp.bool_)
        for k in range(ids_ref.shape[1]):
            member = jnp.logical_or(member, ids_ref[:, k : k + 1] == lane)
        named = member.astype(f32)
        picked = jnp.where(member, probs_ref[...], 0.0)
        total = jnp.sum(picked, axis=1, keepdims=True)
        weight = (picked / total).astype(bf16)
        before = (iota((toks, toks), 0) > iota((toks, toks), 1)).astype(bf16)
        rank = nn(before, named.astype(bf16))
        rank = jnp.where(member, rank, 100.0).astype(bf16)
        rank_s[...] = rank
        w_s[...] = weight
        w_ref[...] = weight.astype(f32)
        sum_ref[...] = jnp.broadcast_to(total, sum_ref.shape)
        count = jnp.sum(named, axis=0, keepdims=True)
        mine = iota(cnt_ref.shape, 0) % CAP == iota(cnt_ref.shape, 1) // (LANES // CAP)
        cnt_ref[...] = jnp.where(mine, jnp.broadcast_to(count, cnt_ref.shape), 0.0)
        slots = pick_ref.shape[1]
        spread_t = (iota((experts, slots), 0) == iota((experts, slots), 1) // CAP).astype(bf16)
        rank_all = nn(rank, spread_t)
        pick_ref[...] = (rank_all == (iota((toks, slots), 1) % CAP).astype(f32)).astype(bf16)

    spread = ((iota((rows, experts), 0) + step * rows) // CAP == iota((rows, experts), 1)).astype(bf16)
    chosen = nt(spread, rank_s[...]) == (iota((rows, toks), 0) % CAP).astype(f32)
    weights = nt(spread, w_s[...])
    x_ref[:, :width] = nn(chosen.astype(bf16), tok_ref[...]).astype(bf16)
    x_ref[:, width:] = nn(jnp.where(chosen, weights, 0.0).astype(bf16), grad_ref[...]).astype(bf16)


def send_rows(ids, probs, tokens, grads):
    toks, width = tokens.shape
    experts = probs.shape[1]
    slots = experts * CAP
    rows = 256
    whole = lambda shape: pl.BlockSpec(shape, lambda i: (0, 0))
    return pl.pallas_call(
        send_kernel,
        grid=(slots // rows,),
        in_specs=[whole(ids.shape), whole(probs.shape), whole(tokens.shape), whole(grads.shape)],
        out_specs=[
            pl.BlockSpec((rows, 2 * width), lambda i: (i, 0)),
            whole((toks, slots)),
            whole((toks, experts)),
            whole((toks, experts)),
            whole((rows, LANES)),
        ],
        out_shape=[
            jax.ShapeDtypeStruct((slots, 2 * width), bf16),
            jax.ShapeDtypeStruct((toks, slots), bf16),
            jax.ShapeDtypeStruct((toks, experts), f32),
            jax.ShapeDtypeStruct((toks, experts), f32),
            jax.ShapeDtypeStruct((rows, LANES), f32),
        ],
        scratch_shapes=[pltpu.VMEM((toks, experts), bf16), pltpu.VMEM((toks, experts), bf16)],
        compiler_params=pltpu.CompilerParams(vmem_limit_bytes=24 << 20),
        name="send_rows",
    )(ids, probs, tokens, grads)


def expert_kernel(tok_ref, grad_ref, gate_ref, up_ref, down_ref, cnt_ref, out_ref, hid_ref, dg_ref, du_ref):
    rows, width = tok_ref.shape
    tok = tok_ref[...]
    gate = nn(tok, gate_ref[...])
    up = nn(tok, up_ref[...])
    back = nt(grad_ref[...], down_ref[...])
    sig = jax.nn.sigmoid(gate)
    silu = gate * sig
    hidden = (silu * up).astype(bf16)
    hid_ref[...] = hidden
    route = jnp.sum(hidden.astype(f32) * back, axis=1, keepdims=True)
    d_gate = (back * up * sig * (1.0 + gate * (1.0 - sig))).astype(bf16)
    d_up = (back * silu).astype(bf16)
    dg_ref[...] = d_gate
    du_ref[...] = d_up
    out_ref[:, :width] = (nt(d_gate, gate_ref[...]) + nt(d_up, up_ref[...])).astype(bf16)
    high = route.astype(bf16).astype(f32)
    turn = (iota((rows, LANES), 1) // (LANES // CAP) - iota((rows, LANES), 0) % CAP + CAP) % CAP
    extra = jnp.where(turn == 4, high, jnp.where(turn == 5, route - high, cnt_ref[...]))
    out_ref[:, width:] = extra.astype(bf16)


def expert_rows(x, gate, up, down, counts):
    slots = x.shape[0]
    width, units = gate.shape
    rows = counts.shape[0]
    whole = lambda shape: pl.BlockSpec(shape, lambda i: (0, 0), pipeline_mode=pl.Buffered(1))
    block = lambda cols, at: pl.BlockSpec((rows, cols), lambda i: (i, at))
    part = jax.ShapeDtypeStruct((slots, units), bf16)
    return pl.pallas_call(
        expert_kernel,
        grid=(slots // rows,),
        in_specs=[
            block(width, 0),
            block(width, 1),
            whole(gate.shape),
            whole(up.shape),
            whole(down.shape),
            whole(counts.shape),
        ],
        out_specs=[block(width + LANES, 0), block(units, 0), block(units, 0), block(units, 0)],
        out_shape=[jax.ShapeDtypeStruct((slots, width + LANES), bf16), part, part, part],
        compiler_params=pltpu.CompilerParams(vmem_limit_bytes=48 << 20),
        name="expert_rows",
    )(x, x, gate, up, down, counts)


def tail_kernel(scale, pick_ref, back_ref, extra_ref, w_ref, sum_ref, tok_ref, prob_ref, acc, route_s, load_s):
    step = pl.program_id(0)
    rows = back_ref.shape[0]
    experts = w_ref.shape[1]

    @pl.when(step == 0)
    def _():
        acc[...] = jnp.zeros_like(acc)
        route_s[...] = jnp.zeros_like(route_s)
        load_s[...] = jnp.zeros_like(load_s)

    pick = pick_ref[...]
    acc[...] += nn(pick, back_ref[...])
    extra = extra_ref[...].astype(f32)
    turn = (iota((rows, LANES), 1) // (LANES // CAP) - iota((rows, LANES), 0) % CAP + CAP) % CAP
    first = iota((rows, LANES), 1) % (LANES // CAP) == 0
    high = jnp.sum(jnp.where(jnp.logical_and(first, turn == 4), extra, 0.0), axis=1, keepdims=True)
    low = jnp.sum(jnp.where(jnp.logical_and(first, turn == 5), extra, 0.0), axis=1, keepdims=True)
    own = (iota((rows, experts), 0) + step * rows) // CAP == iota((rows, experts), 1)
    route_s[...] += nn(pick, jnp.where(own, high, 0.0).astype(bf16)) + nn(
        pick, jnp.where(own, low, 0.0).astype(bf16)
    )
    load_s[...] += jnp.sum(jnp.where(turn == 0, extra, 0.0), axis=0, keepdims=True)

    @pl.when(step == pl.num_programs(0) - 1)
    def _():
        tok_ref[...] = acc[...].astype(bf16)
        weight = w_ref[...]
        named = weight > 0.0
        total = sum_ref[...]
        route = jnp.where(named, route_s[...] / jnp.where(named, weight, 1.0), 0.0)
        route = route.astype(bf16).astype(f32)
        mean = jnp.sum(route * weight, axis=1, keepdims=True)
        prob_ref[...] = jnp.where(named, (route - mean) / total, 0.0) + load_s[...] * scale


def collect_rows(scale, pick, back, weight, total):
    toks, slots = pick.shape
    experts = weight.shape[1]
    width = back.shape[1] - LANES
    rows = 256
    whole = lambda shape: pl.BlockSpec(shape, lambda i: (0, 0))
    return pl.pallas_call(
        lambda *refs: tail_kernel(scale, *refs),
        grid=(slots // rows,),
        in_specs=[
            pl.BlockSpec((toks, rows), lambda i: (0, i)),
            pl.BlockSpec((rows, width), lambda i: (i, 0)),
            pl.BlockSpec((rows, LANES), lambda i: (i, width // LANES)),
            whole(weight.shape),
            whole(total.shape),
        ],
        out_specs=[whole((toks, width)), whole((toks, experts))],
        out_shape=[jax.ShapeDtypeStruct((toks, width), bf16), jax.ShapeDtypeStruct((toks, experts), f32)],
        scratch_shapes=[
            pltpu.VMEM((toks, width), f32),
            pltpu.VMEM((toks, experts), f32),
            pltpu.VMEM((1, LANES), f32),
        ],
        compiler_params=pltpu.CompilerParams(vmem_limit_bytes=24 << 20),
        name="collect_rows",
    )(pick, back, back, weight, total)


def exchange(rows, devices):
    slots, width = rows.shape
    moved = lax.all_to_all(
        rows.reshape(devices, slots // devices, width), AXES, split_axis=0, concat_axis=0, tiled=True
    )
    return moved.reshape(slots, width)


def on_device(tokens, grad_out, probs, expert_ids, w_gate, w_up, w_down):
    toks, width = tokens.shape
    experts = probs.shape[1]
    devices = lax.axis_size("dp") * lax.axis_size("expert")
    x, pick, weight, total, counts = send_rows(expert_ids, probs, tokens, grad_out)
    x = exchange(x, devices)
    out, hidden, d_gate_pre, d_up_pre = expert_rows(x, w_gate[0], w_up[0], w_down[0], counts)
    back = exchange(out, devices)
    d_gate = tn(x[:, :width], d_gate_pre).astype(bf16)
    d_up = tn(x[:, :width], d_up_pre).astype(bf16)
    d_down = tn(hidden, x[:, width:]).astype(bf16)
    scale = aux_weight * experts / (devices * toks * expert_ids.shape[1])
    d_tokens, d_probs = collect_rows(scale, pick, back, weight, total)
    return (d_tokens, d_probs, d_gate[None], d_up[None], d_down[None])


def solution(mesh):
    flat = P(AXES, None)
    deep = P(AXES, None, None)
    return jax.shard_map(
        on_device,
        mesh=mesh,
        in_specs=(flat, flat, flat, flat, deep, deep, deep),
        out_specs=(flat, flat, deep, deep, deep),
        check_vma=False,
    )
```

```python
import jax
import jax.numpy as jnp
from jax import lax
from jax.experimental import pallas as pl
from jax.experimental.pallas import tpu as pltpu
from jax.sharding import PartitionSpec as P

aux_weight = 1.0
CAP = 8
LANES = 128
AXES = ("dp", "expert")
f32 = jnp.float32
bf16 = jnp.bfloat16


def iota(shape, dim):
    return lax.broadcasted_iota(jnp.int32, shape, dim)


def nn(left, right):
    return jnp.dot(left, right, preferred_element_type=f32)


def nt(left, right):
    return lax.dot_general(left, right, (((1,), (1,)), ((), ())), preferred_element_type=f32)


def tn(left, right):
    return lax.dot_general(left, right, (((0,), (0,)), ((), ())), preferred_element_type=f32)


def in_hbm(array):
    return pltpu.with_memory_space_constraint(array, pltpu.HBM)


def in_vmem(array):
    return pltpu.with_memory_space_constraint(array, pltpu.VMEM)


def send_kernel(ids_ref, probs_ref, tok_ref, grad_ref, x_ref, pick_ref, w_ref, sum_ref, cnt_ref, rank_s, w_s):
    step = pl.program_id(0)
    rows = x_ref.shape[0]
    toks, experts = probs_ref.shape
    width = tok_ref.shape[1]

    @pl.when(step == 0)
    def _():
        expert = iota((experts, toks), 0)
        member_t = ids_ref[0:1, :] == expert
        for k in range(1, ids_ref.shape[0]):
            member_t = jnp.logical_or(member_t, ids_ref[k : k + 1, :] == expert)
        same = (iota((experts, experts), 0) == iota((experts, experts), 1)).astype(bf16)
        named = tn(member_t.astype(f32).astype(bf16), same)
        member = named > 0.5
        picked = jnp.where(member, probs_ref[...], 0.0)
        total = jnp.sum(picked, axis=1, keepdims=True)
        weight = (picked / total).astype(bf16)
        before = (iota((toks, toks), 0) > iota((toks, toks), 1)).astype(bf16)
        rank = nn(before, named.astype(bf16))
        rank = jnp.where(member, rank, 100.0).astype(bf16)
        rank_s[...] = rank
        w_s[...] = weight
        w_ref[...] = weight.astype(f32)
        sum_ref[...] = jnp.broadcast_to(total, sum_ref.shape)
        count = jnp.sum(named, axis=0, keepdims=True)
        mine = iota(cnt_ref.shape, 0) % CAP == iota(cnt_ref.shape, 1) // (LANES // CAP)
        cnt_ref[...] = jnp.where(mine, jnp.broadcast_to(count, cnt_ref.shape), 0.0)
        slots = pick_ref.shape[1]
        spread_t = (iota((experts, slots), 0) == iota((experts, slots), 1) // CAP).astype(bf16)
        rank_all = nn(rank, spread_t)
        pick_ref[...] = (rank_all == (iota((toks, slots), 1) % CAP).astype(f32)).astype(bf16)

    spread = ((iota((rows, experts), 0) + step * rows) // CAP == iota((rows, experts), 1)).astype(bf16)
    chosen = nt(spread, rank_s[...]) == (iota((rows, toks), 0) % CAP).astype(f32)
    weights = nt(spread, w_s[...])
    x_ref[:, :width] = nn(chosen.astype(bf16), tok_ref[...]).astype(bf16)
    x_ref[:, width:] = nn(jnp.where(chosen, weights, 0.0).astype(bf16), grad_ref[...]).astype(bf16)


def send_rows(ids, probs, tokens, grads):
    toks, width = tokens.shape
    experts = probs.shape[1]
    slots = experts * CAP
    rows = 256
    whole = lambda shape: pl.BlockSpec(shape, lambda i: (0, 0))
    ids, probs, tokens, grads = [in_hbm(a) for a in (ids.T, probs, tokens, grads)]
    return pl.pallas_call(
        send_kernel,
        grid=(slots // rows,),
        in_specs=[whole(ids.shape), whole(probs.shape), whole(tokens.shape), whole(grads.shape)],
        out_specs=[
            pl.BlockSpec((rows, 2 * width), lambda i: (i, 0)),
            whole((toks, slots)),
            whole((toks, experts)),
            whole((toks, experts)),
            whole((rows, LANES)),
        ],
        out_shape=[
            jax.ShapeDtypeStruct((slots, 2 * width), bf16),
            jax.ShapeDtypeStruct((toks, slots), bf16),
            jax.ShapeDtypeStruct((toks, experts), f32),
            jax.ShapeDtypeStruct((toks, experts), f32),
            jax.ShapeDtypeStruct((rows, LANES), f32),
        ],
        scratch_shapes=[pltpu.VMEM((toks, experts), bf16), pltpu.VMEM((toks, experts), bf16)],
        compiler_params=pltpu.CompilerParams(vmem_limit_bytes=24 << 20),
        name="send_rows",
    )(ids, probs, tokens, grads)


def expert_kernel(tok_ref, grad_ref, gate_ref, up_ref, down_ref, cnt_ref, out_ref, hid_ref, dg_ref, du_ref):
    rows, width = tok_ref.shape
    tok = tok_ref[...]
    gate = nn(tok, gate_ref[...])
    up = nn(tok, up_ref[...])
    back = nt(grad_ref[...], down_ref[...])
    sig = jax.nn.sigmoid(gate)
    silu = gate * sig
    hidden = (silu * up).astype(bf16)
    hid_ref[...] = hidden
    route = jnp.sum(hidden.astype(f32) * back, axis=1, keepdims=True)
    d_gate = (back * up * sig * (1.0 + gate * (1.0 - sig))).astype(bf16)
    d_up = (back * silu).astype(bf16)
    dg_ref[...] = d_gate
    du_ref[...] = d_up
    for at in range(0, width, 512):
        cols = slice(at, at + 512)
        out_ref[:, cols] = (nt(d_gate, gate_ref[cols, :]) + nt(d_up, up_ref[cols, :])).astype(bf16)
    high = route.astype(bf16).astype(f32)
    turn = (iota((rows, LANES), 1) // (LANES // CAP) - iota((rows, LANES), 0) % CAP + CAP) % CAP
    extra = jnp.where(turn == 4, high, jnp.where(turn == 5, route - high, cnt_ref[...]))
    out_ref[:, width:] = extra.astype(bf16)


def expert_rows(x, gate, up, down, counts):
    slots = x.shape[0]
    width, units = gate.shape
    rows = counts.shape[0]
    whole = lambda shape: pl.BlockSpec(shape, lambda i: (0, 0), pipeline_mode=pl.Buffered(1))
    block = lambda cols, at: pl.BlockSpec((rows, cols), lambda i: (i, at))
    part = jax.ShapeDtypeStruct((slots, units), bf16)
    return pl.pallas_call(
        expert_kernel,
        grid=(slots // rows,),
        in_specs=[
            block(width, 0),
            block(width, 1),
            whole(gate.shape),
            whole(up.shape),
            whole(down.shape),
            whole(counts.shape),
        ],
        out_specs=[block(width + LANES, 0), block(units, 0), block(units, 0), block(units, 0)],
        out_shape=[jax.ShapeDtypeStruct((slots, width + LANES), bf16), part, part, part],
        compiler_params=pltpu.CompilerParams(vmem_limit_bytes=50 << 20),
        name="expert_rows",
    )(x, x, gate, up, down, counts)


def tail_kernel(scale, pick_ref, back_ref, extra_ref, w_ref, sum_ref, tok_ref, prob_ref, acc, route_s, load_s):
    step = pl.program_id(0)
    rows = back_ref.shape[0]
    experts = w_ref.shape[1]

    @pl.when(step == 0)
    def _():
        acc[...] = jnp.zeros_like(acc)
        route_s[...] = jnp.zeros_like(route_s)
        load_s[...] = jnp.zeros_like(load_s)

    pick = pick_ref[...]
    acc[...] += nn(pick, back_ref[...])
    extra = extra_ref[...].astype(f32)
    turn = (iota((rows, LANES), 1) // (LANES // CAP) - iota((rows, LANES), 0) % CAP + CAP) % CAP
    first = iota((rows, LANES), 1) % (LANES // CAP) == 0
    high = jnp.sum(jnp.where(jnp.logical_and(first, turn == 4), extra, 0.0), axis=1, keepdims=True)
    low = jnp.sum(jnp.where(jnp.logical_and(first, turn == 5), extra, 0.0), axis=1, keepdims=True)
    own = (iota((rows, experts), 0) + step * rows) // CAP == iota((rows, experts), 1)
    route_s[...] += nn(pick, jnp.where(own, high, 0.0).astype(bf16)) + nn(
        pick, jnp.where(own, low, 0.0).astype(bf16)
    )
    load_s[...] += jnp.sum(jnp.where(turn == 0, extra, 0.0), axis=0, keepdims=True)

    @pl.when(step == pl.num_programs(0) - 1)
    def _():
        tok_ref[...] = acc[...].astype(bf16)
        weight = w_ref[...]
        named = weight > 0.0
        total = sum_ref[...]
        route = jnp.where(named, route_s[...] / jnp.where(named, weight, 1.0), 0.0)
        route = route.astype(bf16).astype(f32)
        mean = jnp.sum(route * weight, axis=1, keepdims=True)
        prob_ref[...] = jnp.where(named, (route - mean) / total, 0.0) + load_s[...] * scale


def collect_rows(scale, pick, back, weight, total):
    toks, slots = pick.shape
    experts = weight.shape[1]
    width = back.shape[1] - LANES
    rows = 256
    whole = lambda shape: pl.BlockSpec(shape, lambda i: (0, 0))
    return pl.pallas_call(
        lambda *refs: tail_kernel(scale, *refs),
        grid=(slots // rows,),
        in_specs=[
            pl.BlockSpec((toks, rows), lambda i: (0, i)),
            pl.BlockSpec((rows, width), lambda i: (i, 0)),
            pl.BlockSpec((rows, LANES), lambda i: (i, width // LANES)),
            whole(weight.shape),
            whole(total.shape),
        ],
        out_specs=[whole((toks, width)), whole((toks, experts))],
        out_shape=[jax.ShapeDtypeStruct((toks, width), bf16), jax.ShapeDtypeStruct((toks, experts), f32)],
        scratch_shapes=[
            pltpu.VMEM((toks, width), f32),
            pltpu.VMEM((toks, experts), f32),
            pltpu.VMEM((1, LANES), f32),
        ],
        compiler_params=pltpu.CompilerParams(vmem_limit_bytes=24 << 20),
        name="collect_rows",
    )(pick, back, back, weight, total)


def exchange(rows, devices):
    slots, width = rows.shape
    moved = lax.all_to_all(
        rows.reshape(devices, slots // devices, width), AXES, split_axis=0, concat_axis=0, tiled=True
    )
    return moved.reshape(slots, width)


def on_device(tokens, grad_out, probs, expert_ids, w_gate, w_up, w_down):
    toks, width = tokens.shape
    experts = probs.shape[1]
    devices = lax.axis_size("dp") * lax.axis_size("expert")
    x, pick, weight, total, counts = send_rows(expert_ids, probs, tokens, grad_out)
    x = exchange(x, devices)
    gate, up, down = [in_vmem(w[0]) for w in (w_gate, w_up, w_down)]
    out, hidden, d_gate_pre, d_up_pre = expert_rows(x, gate, up, down, counts)
    back = exchange(out, devices)
    d_gate = tn(x[:, :width], d_gate_pre).astype(bf16)
    d_up = tn(x[:, :width], d_up_pre).astype(bf16)
    d_down = tn(hidden, x[:, width:]).astype(bf16)
    scale = aux_weight * experts / (devices * toks * expert_ids.shape[1])
    d_tokens, d_probs = collect_rows(scale, pick, back, weight, total)
    return (d_tokens, d_probs, d_gate[None], d_up[None], d_down[None])


def solution(mesh):
    flat = P(AXES, None)
    deep = P(AXES, None, None)
    return jax.shard_map(
        on_device,
        mesh=mesh,
        in_specs=(flat, flat, flat, flat, deep, deep, deep),
        out_specs=(flat, flat, deep, deep, deep),
        check_vma=False,
    )
```

```python
import functools

import jax
import jax.numpy as jnp
from jax import lax
from jax.experimental import pallas as pl
from jax.experimental.pallas import tpu as pltpu
from jax.sharding import PartitionSpec as P

aux_weight = 1.0
CAP = 8
LANES = 128
AXES = ("dp", "expert")
ORDER = ("expert", "dp")
f32 = jnp.float32
bf16 = jnp.bfloat16


def iota(shape, dim):
    return lax.broadcasted_iota(jnp.int32, shape, dim)


def nn(left, right):
    return jnp.dot(left, right, preferred_element_type=f32)


def nt(left, right):
    return lax.dot_general(left, right, (((1,), (1,)), ((), ())), preferred_element_type=f32)


def tn(left, right):
    return lax.dot_general(left, right, (((0,), (0,)), ((), ())), preferred_element_type=f32)


def in_hbm(array):
    return pltpu.with_memory_space_constraint(array, pltpu.HBM)


def in_vmem(array):
    return pltpu.with_memory_space_constraint(array, pltpu.VMEM)


def expert_of(slot, n_data, n_expert):
    block = slot // CAP
    return block % n_data * n_expert + block // n_data


def send_kernel(sizes, ids_ref, probs_ref, tok_ref, grad_ref, x_ref, pick_ref, w_ref, sum_ref, cnt_ref, rank_s, w_s):
    step = pl.program_id(0)
    rows = x_ref.shape[0]
    toks, experts = probs_ref.shape
    width = tok_ref.shape[1]

    @pl.when(step == 0)
    def _():
        expert = iota((experts, toks), 0)
        member_t = ids_ref[0:1, :] == expert
        for k in range(1, ids_ref.shape[0]):
            member_t = jnp.logical_or(member_t, ids_ref[k : k + 1, :] == expert)
        same = (iota((experts, experts), 0) == iota((experts, experts), 1)).astype(bf16)
        named = tn(member_t.astype(f32).astype(bf16), same)
        member = named > 0.5
        picked = jnp.where(member, probs_ref[...], 0.0)
        total = jnp.sum(picked, axis=1, keepdims=True)
        weight = (picked / total).astype(bf16)
        before = (iota((toks, toks), 0) > iota((toks, toks), 1)).astype(bf16)
        rank = nn(before, named.astype(bf16))
        rank = jnp.where(member, rank, 100.0).astype(bf16)
        rank_s[...] = rank
        w_s[...] = weight
        w_ref[...] = weight.astype(f32)
        sum_ref[...] = jnp.broadcast_to(total, sum_ref.shape)
        count = jnp.sum(named, axis=0, keepdims=True)
        mine = iota(cnt_ref.shape, 0) % CAP == iota(cnt_ref.shape, 1) // (LANES // CAP)
        cnt_ref[...] = jnp.where(mine, jnp.broadcast_to(count, cnt_ref.shape), 0.0)
        slots = pick_ref.shape[1]
        spread_t = (iota((experts, slots), 0) == expert_of(iota((experts, slots), 1), *sizes)).astype(bf16)
        rank_all = nn(rank, spread_t)
        pick_ref[...] = (rank_all == (iota((toks, slots), 1) % CAP).astype(f32)).astype(bf16)

    slot = iota((rows, experts), 0) + step * rows
    spread = (expert_of(slot, *sizes) == iota((rows, experts), 1)).astype(bf16)
    chosen = nt(spread, rank_s[...]) == (iota((rows, toks), 0) % CAP).astype(f32)
    weights = nt(spread, w_s[...])
    x_ref[:, :width] = nn(chosen.astype(bf16), tok_ref[...]).astype(bf16)
    x_ref[:, width:] = nn(jnp.where(chosen, weights, 0.0).astype(bf16), grad_ref[...]).astype(bf16)


def send_rows(sizes, ids, probs, tokens, grads):
    toks, width = tokens.shape
    experts = probs.shape[1]
    slots = experts * CAP
    rows = 256
    whole = lambda shape: pl.BlockSpec(shape, lambda i: (0, 0))
    ids, probs, tokens, grads = [in_hbm(a) for a in (ids.T, probs, tokens, grads)]
    return pl.pallas_call(
        functools.partial(send_kernel, sizes),
        grid=(slots // rows,),
        in_specs=[whole(ids.shape), whole(probs.shape), whole(tokens.shape), whole(grads.shape)],
        out_specs=[
            pl.BlockSpec((rows, 2 * width), lambda i: (i, 0)),
            whole((toks, slots)),
            whole((toks, experts)),
            whole((toks, experts)),
            whole((rows, LANES)),
        ],
        out_shape=[
            jax.ShapeDtypeStruct((slots, 2 * width), bf16),
            jax.ShapeDtypeStruct((toks, slots), bf16),
            jax.ShapeDtypeStruct((toks, experts), f32),
            jax.ShapeDtypeStruct((toks, experts), f32),
            jax.ShapeDtypeStruct((rows, LANES), f32),
        ],
        scratch_shapes=[pltpu.VMEM((toks, experts), bf16), pltpu.VMEM((toks, experts), bf16)],
        compiler_params=pltpu.CompilerParams(vmem_limit_bytes=24 << 20),
        name="send_rows",
    )(ids, probs, tokens, grads)


def expert_kernel(tok_ref, grad_ref, gate_ref, up_ref, down_ref, cnt_ref, out_ref, hid_ref, dg_ref, du_ref):
    rows, width = tok_ref.shape
    units = hid_ref.shape[1]
    route = jnp.zeros((rows, 1), f32)
    for at in range(0, units, 256):
        part = slice(at, at + 256)
        gate = nn(tok_ref[...], gate_ref[:, part])
        up = nn(tok_ref[...], up_ref[:, part])
        back = nt(grad_ref[...], down_ref[part, :])
        sig = jax.nn.sigmoid(gate)
        silu = gate * sig
        hidden = (silu * up).astype(bf16)
        hid_ref[:, part] = hidden
        route += jnp.sum(hidden.astype(f32) * back, axis=1, keepdims=True)
        dg_ref[:, part] = (back * up * sig * (1.0 + gate * (1.0 - sig))).astype(bf16)
        du_ref[:, part] = (back * silu).astype(bf16)
    d_gate = dg_ref[...]
    d_up = du_ref[...]
    for at in range(0, width, 512):
        cols = slice(at, at + 512)
        out_ref[:, cols] = (nt(d_gate, gate_ref[cols, :]) + nt(d_up, up_ref[cols, :])).astype(bf16)
    high = route.astype(bf16).astype(f32)
    turn = (iota((rows, LANES), 1) // (LANES // CAP) - iota((rows, LANES), 0) % CAP + CAP) % CAP
    extra = jnp.where(turn == 4, high, jnp.where(turn == 5, route - high, cnt_ref[...]))
    out_ref[:, width:] = extra.astype(bf16)


def expert_rows(x, gate, up, down, counts):
    slots = x.shape[0]
    width, units = gate.shape
    rows = counts.shape[0]
    whole = lambda shape: pl.BlockSpec(shape, lambda i: (0, 0), pipeline_mode=pl.Buffered(1))
    block = lambda cols, at: pl.BlockSpec((rows, cols), lambda i: (i, at))
    part = jax.ShapeDtypeStruct((slots, units), bf16)
    return pl.pallas_call(
        expert_kernel,
        grid=(slots // rows,),
        in_specs=[
            block(width, 0),
            block(width, 1),
            whole(gate.shape),
            whole(up.shape),
            whole(down.shape),
            whole(counts.shape),
        ],
        out_specs=[block(width + LANES, 0), block(units, 0), block(units, 0), block(units, 0)],
        out_shape=[jax.ShapeDtypeStruct((slots, width + LANES), bf16), part, part, part],
        compiler_params=pltpu.CompilerParams(vmem_limit_bytes=50 << 20),
        name="expert_rows",
    )(x, x, gate, up, down, counts)


def tail_kernel(sizes, scale, pick_ref, back_ref, extra_ref, w_ref, sum_ref, tok_ref, prob_ref, acc, route_s, load_s):
    step = pl.program_id(0)
    rows = back_ref.shape[0]
    experts = w_ref.shape[1]

    @pl.when(step == 0)
    def _():
        acc[...] = jnp.zeros_like(acc)
        route_s[...] = jnp.zeros_like(route_s)
        load_s[...] = jnp.zeros_like(load_s)

    pick = pick_ref[...]
    acc[...] += nn(pick, back_ref[...])
    extra = extra_ref[...].astype(f32)
    turn = (iota((rows, LANES), 1) // (LANES // CAP) - iota((rows, LANES), 0) % CAP + CAP) % CAP
    first = iota((rows, LANES), 1) % (LANES // CAP) == 0
    high = jnp.sum(jnp.where(jnp.logical_and(first, turn == 4), extra, 0.0), axis=1, keepdims=True)
    low = jnp.sum(jnp.where(jnp.logical_and(first, turn == 5), extra, 0.0), axis=1, keepdims=True)
    slot = iota((rows, experts), 0) + step * rows
    own = expert_of(slot, *sizes) == iota((rows, experts), 1)
    route_s[...] += nn(pick, jnp.where(own, high, 0.0).astype(bf16)) + nn(
        pick, jnp.where(own, low, 0.0).astype(bf16)
    )
    load_s[...] += jnp.sum(jnp.where(turn == 0, extra, 0.0), axis=0, keepdims=True)

    @pl.when(step == pl.num_programs(0) - 1)
    def _():
        tok_ref[...] = acc[...].astype(bf16)
        weight = w_ref[...]
        named = weight > 0.0
        total = sum_ref[...]
        route = jnp.where(named, route_s[...] / jnp.where(named, weight, 1.0), 0.0)
        route = route.astype(bf16).astype(f32)
        mean = jnp.sum(route * weight, axis=1, keepdims=True)
        prob_ref[...] = jnp.where(named, (route - mean) / total, 0.0) + load_s[...] * scale


def collect_rows(sizes, scale, pick, back, weight, total):
    toks, slots = pick.shape
    experts = weight.shape[1]
    width = back.shape[1] - LANES
    rows = 256
    whole = lambda shape: pl.BlockSpec(shape, lambda i: (0, 0))
    return pl.pallas_call(
        functools.partial(tail_kernel, sizes, scale),
        grid=(slots // rows,),
        in_specs=[
            pl.BlockSpec((toks, rows), lambda i: (0, i)),
            pl.BlockSpec((rows, width), lambda i: (i, 0)),
            pl.BlockSpec((rows, LANES), lambda i: (i, width // LANES)),
            whole(weight.shape),
            whole(total.shape),
        ],
        out_specs=[whole((toks, width)), whole((toks, experts))],
        out_shape=[jax.ShapeDtypeStruct((toks, width), bf16), jax.ShapeDtypeStruct((toks, experts), f32)],
        scratch_shapes=[
            pltpu.VMEM((toks, width), f32),
            pltpu.VMEM((toks, experts), f32),
            pltpu.VMEM((1, LANES), f32),
        ],
        compiler_params=pltpu.CompilerParams(vmem_limit_bytes=24 << 20),
        name="collect_rows",
    )(pick, back, back, weight, total)


def exchange(rows, devices):
    slots, width = rows.shape
    moved = lax.all_to_all(
        rows.reshape(devices, slots // devices, width), ORDER, split_axis=0, concat_axis=0, tiled=True
    )
    return moved.reshape(slots, width)


def on_device(tokens, grad_out, probs, expert_ids, w_gate, w_up, w_down):
    toks, width = tokens.shape
    experts = probs.shape[1]
    sizes = (lax.axis_size("dp"), lax.axis_size("expert"))
    devices = sizes[0] * sizes[1]
    x, pick, weight, total, counts = send_rows(sizes, expert_ids, probs, tokens, grad_out)
    x = exchange(x, devices)
    gate, up, down = [in_vmem(w[0]) for w in (w_gate, w_up, w_down)]
    out, hidden, d_gate_pre, d_up_pre = expert_rows(x, gate, up, down, counts)
    back = exchange(out, devices)
    d_gate = tn(x[:, :width], d_gate_pre).astype(bf16)
    d_up = tn(x[:, :width], d_up_pre).astype(bf16)
    d_down = tn(hidden, x[:, width:]).astype(bf16)
    scale = aux_weight * experts / (devices * toks * expert_ids.shape[1])
    d_tokens, d_probs = collect_rows(sizes, scale, pick, back, weight, total)
    return (d_tokens, d_probs, d_gate[None], d_up[None], d_down[None])


def solution(mesh):
    flat = P(AXES, None)
    deep = P(AXES, None, None)
    return jax.shard_map(
        on_device,
        mesh=mesh,
        in_specs=(flat, flat, flat, flat, deep, deep, deep),
        out_specs=(flat, flat, deep, deep, deep),
        check_vma=False,
    )
```

```python
import functools

import jax
import jax.numpy as jnp
from jax import lax
from jax.experimental import pallas as pl
from jax.experimental.pallas import tpu as pltpu
from jax.sharding import PartitionSpec as P

aux_weight = 1.0
CAP = 8
LANES = 128
ROWS = 256
AXES = ("dp", "expert")
f32 = jnp.float32
bf16 = jnp.bfloat16


def iota(shape, dim):
    return lax.broadcasted_iota(jnp.int32, shape, dim)


def nn(left, right):
    return jnp.dot(left, right, preferred_element_type=f32)


def nt(left, right):
    return lax.dot_general(left, right, (((1,), (1,)), ((), ())), preferred_element_type=f32)


def tn(left, right):
    return lax.dot_general(left, right, (((0,), (0,)), ((), ())), preferred_element_type=f32)


def in_hbm(array):
    return pltpu.with_memory_space_constraint(array, pltpu.HBM)


def in_vmem(array):
    return pltpu.with_memory_space_constraint(array, pltpu.VMEM)


def send_kernel(
    ids_hbm, probs_hbm, tok_hbm, grad_hbm, x_ref, pick_ref, w_ref, sum_ref, cnt_ref, ids_ref, probs_ref, tok_ref, grad_ref, sems
):
    toks, experts = probs_ref.shape
    slots, width = x_ref.shape[0], tok_ref.shape[1]
    pairs = ((ids_hbm, ids_ref), (probs_hbm, probs_ref), (tok_hbm, tok_ref), (grad_hbm, grad_ref))
    copies = [pltpu.make_async_copy(a, b, sems.at[i]) for i, (a, b) in enumerate(pairs)]
    for copy in copies:
        copy.start()

    copies[0].wait()
    expert = iota((experts, toks), 0)
    member_t = ids_ref[0:1, :] == expert
    for k in range(1, ids_ref.shape[0]):
        member_t = jnp.logical_or(member_t, ids_ref[k : k + 1, :] == expert)
    same = (iota((experts, experts), 0) == iota((experts, experts), 1)).astype(bf16)
    named = tn(member_t.astype(f32).astype(bf16), same)
    member = named > 0.5
    before = (iota((toks, toks), 0) > iota((toks, toks), 1)).astype(bf16)
    rank = nn(before, named.astype(bf16))
    rank = jnp.where(member, rank, 100.0).astype(bf16)
    copies[1].wait()
    picked = jnp.where(member, probs_ref[...], 0.0)
    total = jnp.sum(picked, axis=1, keepdims=True)
    weight = (picked / total).astype(bf16)

    w_ref[...] = weight.astype(f32)
    sum_ref[...] = jnp.broadcast_to(total, sum_ref.shape)
    count = jnp.sum(named, axis=0, keepdims=True)
    mine = iota(cnt_ref.shape, 0) % CAP == iota(cnt_ref.shape, 1) // (LANES // CAP)
    cnt_ref[...] = jnp.where(mine, jnp.broadcast_to(count, cnt_ref.shape), 0.0)
    spread_t = (iota((experts, slots), 0) == iota((experts, slots), 1) // CAP).astype(bf16)
    pick_ref[...] = (nn(rank, spread_t) == (iota((toks, slots), 1) % CAP).astype(f32)).astype(bf16)

    spread = (iota((slots, experts), 0) // CAP == iota((slots, experts), 1)).astype(bf16)
    chosen = nt(spread, rank) == (iota((slots, toks), 0) % CAP).astype(f32)
    weights = nt(spread, weight)
    weights = jnp.where(chosen, weights, 0.0).astype(bf16)
    chosen = chosen.astype(bf16)
    copies[2].wait()
    copies[3].wait()
    for at in range(0, width, 512):
        x_ref[:, at : at + 512] = nn(chosen, tok_ref[:, at : at + 512]).astype(bf16)
        x_ref[:, width + at : width + at + 512] = nn(weights, grad_ref[:, at : at + 512]).astype(bf16)


def send_rows(ids, probs, tokens, grads):
    toks, width = tokens.shape
    experts = probs.shape[1]
    slots = experts * CAP
    arrays = [in_hbm(a) for a in (ids.T, probs, tokens, grads)]
    return pl.pallas_call(
        send_kernel,
        in_specs=[pl.BlockSpec(memory_space=pltpu.HBM)] * 4,
        out_specs=[pl.BlockSpec(memory_space=pltpu.VMEM)] * 5,
        out_shape=[
            jax.ShapeDtypeStruct((slots, 2 * width), bf16),
            jax.ShapeDtypeStruct((toks, slots), bf16),
            jax.ShapeDtypeStruct((toks, experts), f32),
            jax.ShapeDtypeStruct((toks, experts), f32),
            jax.ShapeDtypeStruct((ROWS, LANES), f32),
        ],
        scratch_shapes=[pltpu.VMEM(a.shape, a.dtype) for a in arrays] + [pltpu.SemaphoreType.DMA((4,))],
        compiler_params=pltpu.CompilerParams(vmem_limit_bytes=24 << 20),
        name="send_rows",
    )(*arrays)


def expert_kernel(tok_ref, grad_ref, gate_ref, up_ref, down_ref, cnt_ref, out_ref, hid_ref, dg_ref, du_ref):
    rows, width = tok_ref.shape
    units = hid_ref.shape[1]
    route = jnp.zeros((rows, 1), f32)
    for at in range(0, units, 256):
        part = slice(at, at + 256)
        gate = nn(tok_ref[...], gate_ref[:, part])
        up = nn(tok_ref[...], up_ref[:, part])
        back = nt(grad_ref[...], down_ref[part, :])
        sig = jax.nn.sigmoid(gate)
        silu = gate * sig
        hidden = (silu * up).astype(bf16)
        hid_ref[:, part] = hidden
        route += jnp.sum(hidden.astype(f32) * back, axis=1, keepdims=True)
        dg_ref[:, part] = (back * up * sig * (1.0 + gate * (1.0 - sig))).astype(bf16)
        du_ref[:, part] = (back * silu).astype(bf16)
    d_gate = dg_ref[...]
    d_up = du_ref[...]
    for at in range(0, width, 512):
        cols = slice(at, at + 512)
        out_ref[:, cols] = (nt(d_gate, gate_ref[cols, :]) + nt(d_up, up_ref[cols, :])).astype(bf16)
    high = route.astype(bf16).astype(f32)
    turn = (iota((rows, LANES), 1) // (LANES // CAP) - iota((rows, LANES), 0) % CAP + CAP) % CAP
    extra = jnp.where(turn == 4, high, jnp.where(turn == 5, route - high, cnt_ref[...]))
    out_ref[:, width:] = extra.astype(bf16)


def expert_rows(x, gate, up, down, counts):
    slots = x.shape[0]
    width, units = gate.shape
    rows = counts.shape[0]
    whole = lambda shape: pl.BlockSpec(shape, lambda i: (0, 0), pipeline_mode=pl.Buffered(1))
    block = lambda cols, at: pl.BlockSpec((rows, cols), lambda i: (i, at))
    part = jax.ShapeDtypeStruct((slots, units), bf16)
    return pl.pallas_call(
        expert_kernel,
        grid=(slots // rows,),
        in_specs=[
            block(width, 0),
            block(width, 1),
            whole(gate.shape),
            whole(up.shape),
            whole(down.shape),
            whole(counts.shape),
        ],
        out_specs=[block(width + LANES, 0), block(units, 0), block(units, 0), block(units, 0)],
        out_shape=[jax.ShapeDtypeStruct((slots, width + LANES), bf16), part, part, part],
        compiler_params=pltpu.CompilerParams(vmem_limit_bytes=50 << 20),
        name="expert_rows",
    )(x, x, gate, up, down, counts)


def tail_kernel(scale, pick_ref, w_ref, sum_ref, back_hbm, tok_ref, prob_ref, back_ref, acc, sems):
    slots, width = back_ref.shape[0], tok_ref.shape[1]
    experts = w_ref.shape[1]
    blocks = [pl.ds(at, ROWS) for at in range(0, slots, ROWS)]
    copies = [pltpu.make_async_copy(back_hbm.at[b], back_ref.at[b], sems.at[i]) for i, b in enumerate(blocks)]
    for copy in copies:
        copy.start()

    turn = (iota((ROWS, LANES), 1) // (LANES // CAP) - iota((ROWS, LANES), 0) % CAP + CAP) % CAP
    first = iota((ROWS, LANES), 1) % (LANES // CAP) == 0
    is_high = jnp.logical_and(first, turn == 4)
    is_low = jnp.logical_and(first, turn == 5)
    route = jnp.zeros(w_ref.shape, f32)
    load = jnp.zeros((1, LANES), f32)
    for i, block in enumerate(blocks):
        copies[i].wait()
        pick = pick_ref[:, i * ROWS : (i + 1) * ROWS]
        extra = back_ref[block, width:].astype(f32)
        high = jnp.sum(jnp.where(is_high, extra, 0.0), axis=1, keepdims=True)
        low = jnp.sum(jnp.where(is_low, extra, 0.0), axis=1, keepdims=True)
        own = (iota((ROWS, experts), 0) + i * ROWS) // CAP == iota((ROWS, experts), 1)
        route += nn(pick, jnp.where(own, high, 0.0).astype(bf16)) + nn(pick, jnp.where(own, low, 0.0).astype(bf16))
        load += jnp.sum(jnp.where(turn == 0, extra, 0.0), axis=0, keepdims=True)
        rows = nn(pick, back_ref[block, :width])
        if i == 0:
            acc[...] = rows
        elif i < len(blocks) - 1:
            acc[...] += rows
        else:
            tok_ref[...] = (acc[...] + rows).astype(bf16)
    weight = w_ref[...]
    member = weight > 0.0
    route = jnp.where(member, route / jnp.where(member, weight, 1.0), 0.0)
    route = route.astype(bf16).astype(f32)
    mean = jnp.sum(route * weight, axis=1, keepdims=True)
    prob_ref[...] = jnp.where(member, (route - mean) / sum_ref[...], 0.0) + load * scale


def collect_rows(scale, pick, back, weight, total):
    toks, slots = pick.shape
    experts = weight.shape[1]
    width = back.shape[1] - LANES
    return pl.pallas_call(
        functools.partial(tail_kernel, scale),
        in_specs=[pl.BlockSpec(memory_space=pltpu.VMEM)] * 3 + [pl.BlockSpec(memory_space=pltpu.HBM)],
        out_specs=[pl.BlockSpec(memory_space=pltpu.VMEM)] * 2,
        out_shape=[jax.ShapeDtypeStruct((toks, width), bf16), jax.ShapeDtypeStruct((toks, experts), f32)],
        scratch_shapes=[
            pltpu.VMEM(back.shape, bf16),
            pltpu.VMEM((toks, width), f32),
            pltpu.SemaphoreType.DMA((slots // ROWS,)),
        ],
        compiler_params=pltpu.CompilerParams(vmem_limit_bytes=24 << 20),
        name="collect_rows",
    )(pick, weight, total, in_hbm(back))


def exchange(rows, devices):
    slots, width = rows.shape
    moved = lax.all_to_all(
        rows.reshape(devices, slots // devices, width), AXES, split_axis=0, concat_axis=0, tiled=True
    )
    return moved.reshape(slots, width)


def on_device(tokens, grad_out, probs, expert_ids, w_gate, w_up, w_down):
    toks, width = tokens.shape
    experts = probs.shape[1]
    devices = lax.axis_size("dp") * lax.axis_size("expert")
    x, pick, weight, total, counts = send_rows(expert_ids, probs, tokens, grad_out)
    x = exchange(x, devices)
    gate, up, down = [in_vmem(w[0]) for w in (w_gate, w_up, w_down)]
    out, hidden, d_gate_pre, d_up_pre = expert_rows(x, gate, up, down, counts)
    back = exchange(out, devices)
    d_gate = tn(x[:, :width], d_gate_pre).astype(bf16)
    d_up = tn(x[:, :width], d_up_pre).astype(bf16)
    d_down = tn(hidden, x[:, width:]).astype(bf16)
    scale = aux_weight * experts / (devices * toks * expert_ids.shape[1])
    d_tokens, d_probs = collect_rows(scale, pick, back, weight, total)
    return (d_tokens, d_probs, d_gate[None], d_up[None], d_down[None])


def solution(mesh):
    flat = P(AXES, None)
    deep = P(AXES, None, None)
    return jax.shard_map(
        on_device,
        mesh=mesh,
        in_specs=(flat, flat, flat, flat, deep, deep, deep),
        out_specs=(flat, flat, deep, deep, deep),
        check_vma=False,
    )
```

```python
import functools

import jax
import jax.numpy as jnp
from jax import lax
from jax.experimental import pallas as pl
from jax.experimental.pallas import tpu as pltpu
from jax.sharding import PartitionSpec as P

aux_weight = 1.0
CAP = 8
LANES = 128
ROWS = 256
AXES = ("dp", "expert")
f32 = jnp.float32
bf16 = jnp.bfloat16


def iota(shape, dim):
    return lax.broadcasted_iota(jnp.int32, shape, dim)


def nn(left, right):
    return jnp.dot(left, right, preferred_element_type=f32)


def nt(left, right):
    return lax.dot_general(left, right, (((1,), (1,)), ((), ())), preferred_element_type=f32)


def tn(left, right):
    return lax.dot_general(left, right, (((0,), (0,)), ((), ())), preferred_element_type=f32)


def in_hbm(array):
    return pltpu.with_memory_space_constraint(array, pltpu.HBM)


def in_vmem(array):
    return pltpu.with_memory_space_constraint(array, pltpu.VMEM)


def send_kernel(
    ids_hbm, probs_hbm, tok_hbm, grad_hbm, x_ref, pick_ref, w_ref, sum_ref, cnt_ref, ids_ref, probs_ref, tok_ref, grad_ref, sems
):
    toks, experts = probs_ref.shape
    slots, width = x_ref.shape[0], tok_ref.shape[1]
    pairs = ((ids_hbm, ids_ref), (probs_hbm, probs_ref), (tok_hbm, tok_ref), (grad_hbm, grad_ref))
    copies = [pltpu.make_async_copy(a, b, sems.at[i]) for i, (a, b) in enumerate(pairs)]
    for copy in copies:
        copy.start()

    copies[0].wait()
    expert = iota((experts, toks), 0)
    member_t = ids_ref[0:1, :] == expert
    for k in range(1, ids_ref.shape[0]):
        member_t = jnp.logical_or(member_t, ids_ref[k : k + 1, :] == expert)
    same = (iota((experts, experts), 0) == iota((experts, experts), 1)).astype(bf16)
    named = tn(member_t.astype(f32).astype(bf16), same)
    member = named > 0.5
    before = (iota((toks, toks), 0) > iota((toks, toks), 1)).astype(bf16)
    rank = nn(before, named.astype(bf16))
    rank = jnp.where(member, rank, 100.0).astype(bf16)
    copies[1].wait()
    picked = jnp.where(member, probs_ref[...], 0.0)
    total = jnp.sum(picked, axis=1, keepdims=True)
    weight = (picked / total).astype(bf16)

    w_ref[...] = weight.astype(f32)
    sum_ref[...] = jnp.broadcast_to(total, sum_ref.shape)
    count = jnp.sum(named, axis=0, keepdims=True)
    mine = iota(cnt_ref.shape, 0) % CAP == iota(cnt_ref.shape, 1) // (LANES // CAP)
    cnt_ref[...] = jnp.where(mine, jnp.broadcast_to(count, cnt_ref.shape), 0.0)
    spread_t = (iota((experts, slots), 0) == iota((experts, slots), 1) // CAP).astype(bf16)
    pick_ref[...] = (nn(rank, spread_t) == (iota((toks, slots), 1) % CAP).astype(f32)).astype(bf16)

    spread = (iota((slots, experts), 0) // CAP == iota((slots, experts), 1)).astype(bf16)
    chosen = nt(spread, rank) == (iota((slots, toks), 0) % CAP).astype(f32)
    weights = nt(spread, weight)
    weights = jnp.where(chosen, weights, 0.0).astype(bf16)
    chosen = chosen.astype(bf16)
    copies[2].wait()
    copies[3].wait()
    for at in range(0, width, 512):
        x_ref[:, at : at + 512] = nn(chosen, tok_ref[:, at : at + 512]).astype(bf16)
        x_ref[:, width + at : width + at + 512] = nn(weights, grad_ref[:, at : at + 512]).astype(bf16)


def send_rows(ids, probs, tokens, grads):
    toks, width = tokens.shape
    experts = probs.shape[1]
    slots = experts * CAP
    arrays = [in_hbm(a) for a in (ids.T, probs, tokens, grads)]
    return pl.pallas_call(
        send_kernel,
        in_specs=[pl.BlockSpec(memory_space=pltpu.HBM)] * 4,
        out_specs=[pl.BlockSpec(memory_space=pltpu.VMEM)] * 5,
        out_shape=[
            jax.ShapeDtypeStruct((slots, 2 * width), bf16),
            jax.ShapeDtypeStruct((toks, slots), bf16),
            jax.ShapeDtypeStruct((toks, experts), f32),
            jax.ShapeDtypeStruct((toks, experts), f32),
            jax.ShapeDtypeStruct((ROWS, LANES), f32),
        ],
        scratch_shapes=[pltpu.VMEM(a.shape, a.dtype) for a in arrays] + [pltpu.SemaphoreType.DMA((4,))],
        compiler_params=pltpu.CompilerParams(vmem_limit_bytes=24 << 20),
        name="send_rows",
    )(*arrays)


def expert_kernel(tok_ref, grad_ref, gate_ref, up_ref, down_ref, cnt_ref, out_ref, hid_ref, dg_ref, du_ref):
    rows, width = tok_ref.shape
    units = hid_ref.shape[1]
    terms = jnp.zeros((rows, LANES), f32)
    for at in range(0, units, 256):
        part = slice(at, at + 256)
        gate = nn(tok_ref[...], gate_ref[:, part])
        up = nn(tok_ref[...], up_ref[:, part])
        back = nt(grad_ref[...], down_ref[part, :])
        sig = jax.nn.sigmoid(gate)
        silu = gate * sig
        hidden = (silu * up).astype(bf16)
        hid_ref[:, part] = hidden
        term = hidden.astype(f32) * back
        terms += term[:, :LANES] + term[:, LANES:]
        dg_ref[:, part] = (back * up * sig * (1.0 + gate * (1.0 - sig))).astype(bf16)
        du_ref[:, part] = (back * silu).astype(bf16)
    d_gate = dg_ref[...]
    d_up = du_ref[...]
    for at in range(0, width, 512):
        cols = slice(at, at + 512)
        out_ref[:, cols] = (nt(d_gate, gate_ref[cols, :]) + nt(d_up, up_ref[cols, :])).astype(bf16)
    route = jnp.sum(terms, axis=1, keepdims=True)
    high = route.astype(bf16).astype(f32)
    turn = (iota((rows, LANES), 1) // (LANES // CAP) - iota((rows, LANES), 0) % CAP + CAP) % CAP
    extra = jnp.where(turn == 4, high, jnp.where(turn == 5, route - high, cnt_ref[...]))
    out_ref[:, width:] = extra.astype(bf16)


def expert_rows(x, gate, up, down, counts):
    slots = x.shape[0]
    width, units = gate.shape
    rows = counts.shape[0]
    whole = lambda shape: pl.BlockSpec(shape, lambda i: (0, 0), pipeline_mode=pl.Buffered(1))
    block = lambda cols, at: pl.BlockSpec((rows, cols), lambda i: (i, at))
    part = jax.ShapeDtypeStruct((slots, units), bf16)
    return pl.pallas_call(
        expert_kernel,
        grid=(slots // rows,),
        in_specs=[
            block(width, 0),
            block(width, 1),
            whole(gate.shape),
            whole(up.shape),
            whole(down.shape),
            whole(counts.shape),
        ],
        out_specs=[block(width + LANES, 0), block(units, 0), block(units, 0), block(units, 0)],
        out_shape=[jax.ShapeDtypeStruct((slots, width + LANES), bf16), part, part, part],
        compiler_params=pltpu.CompilerParams(vmem_limit_bytes=41 << 20),
        name="expert_rows",
    )(x, x, gate, up, down, counts)


def tail_kernel(scale, pick_ref, w_ref, sum_ref, back_hbm, tok_ref, prob_ref, back_ref, acc, sems):
    slots, width = back_ref.shape[0], tok_ref.shape[1]
    experts = w_ref.shape[1]
    blocks = [pl.ds(at, ROWS) for at in range(0, slots, ROWS)]
    copies = [pltpu.make_async_copy(back_hbm.at[b], back_ref.at[b], sems.at[i]) for i, b in enumerate(blocks)]
    for copy in copies:
        copy.start()

    turn = (iota((ROWS, LANES), 1) // (LANES // CAP) - iota((ROWS, LANES), 0) % CAP + CAP) % CAP
    first = iota((ROWS, LANES), 1) % (LANES // CAP) == 0
    is_high = jnp.logical_and(first, turn == 4)
    is_low = jnp.logical_and(first, turn == 5)
    route = jnp.zeros(w_ref.shape, f32)
    load = jnp.zeros((1, LANES), f32)
    for i, block in enumerate(blocks):
        copies[i].wait()
        pick = pick_ref[:, i * ROWS : (i + 1) * ROWS]
        extra = back_ref[block, width:].astype(f32)
        high = jnp.sum(jnp.where(is_high, extra, 0.0), axis=1, keepdims=True)
        low = jnp.sum(jnp.where(is_low, extra, 0.0), axis=1, keepdims=True)
        own = (iota((ROWS, experts), 0) + i * ROWS) // CAP == iota((ROWS, experts), 1)
        route += nn(pick, jnp.where(own, high, 0.0).astype(bf16)) + nn(pick, jnp.where(own, low, 0.0).astype(bf16))
        load += jnp.sum(jnp.where(turn == 0, extra, 0.0), axis=0, keepdims=True)
        rows = nn(pick, back_ref[block, :width])
        if i == 0:
            acc[...] = rows
        elif i < len(blocks) - 1:
            acc[...] += rows
        else:
            tok_ref[...] = (acc[...] + rows).astype(bf16)
    weight = w_ref[...]
    member = weight > 0.0
    route = jnp.where(member, route / jnp.where(member, weight, 1.0), 0.0)
    route = route.astype(bf16).astype(f32)
    mean = jnp.sum(route * weight, axis=1, keepdims=True)
    prob_ref[...] = jnp.where(member, (route - mean) / sum_ref[...], 0.0) + load * scale


def collect_rows(scale, pick, back, weight, total):
    toks, slots = pick.shape
    experts = weight.shape[1]
    width = back.shape[1] - LANES
    return pl.pallas_call(
        functools.partial(tail_kernel, scale),
        in_specs=[pl.BlockSpec(memory_space=pltpu.VMEM)] * 3 + [pl.BlockSpec(memory_space=pltpu.HBM)],
        out_specs=[pl.BlockSpec(memory_space=pltpu.VMEM)] * 2,
        out_shape=[jax.ShapeDtypeStruct((toks, width), bf16), jax.ShapeDtypeStruct((toks, experts), f32)],
        scratch_shapes=[
            pltpu.VMEM(back.shape, bf16),
            pltpu.VMEM((toks, width), f32),
            pltpu.SemaphoreType.DMA((slots // ROWS,)),
        ],
        compiler_params=pltpu.CompilerParams(vmem_limit_bytes=24 << 20),
        name="collect_rows",
    )(pick, weight, total, in_hbm(back))


def exchange(rows, devices):
    slots, width = rows.shape
    moved = lax.all_to_all(
        rows.reshape(devices, slots // devices, width), AXES, split_axis=0, concat_axis=0, tiled=True
    )
    return moved.reshape(slots, width)


def on_device(tokens, grad_out, probs, expert_ids, w_gate, w_up, w_down):
    toks, width = tokens.shape
    experts = probs.shape[1]
    devices = lax.axis_size("dp") * lax.axis_size("expert")
    x, pick, weight, total, counts = send_rows(expert_ids, probs, tokens, grad_out)
    x = exchange(x, devices)
    gate, up, down = [in_vmem(w[0]) for w in (w_gate, w_up, w_down)]
    out, hidden, d_gate_pre, d_up_pre = expert_rows(x, gate, up, down, counts)
    back = exchange(out, devices)
    d_gate = tn(x[:, :width], d_gate_pre).astype(bf16)
    d_up = tn(x[:, :width], d_up_pre).astype(bf16)
    d_down = tn(hidden, x[:, width:]).astype(bf16)
    scale = aux_weight * experts / (devices * toks * expert_ids.shape[1])
    d_tokens, d_probs = collect_rows(scale, pick, back, weight, total)
    return (d_tokens, d_probs, d_gate[None], d_up[None], d_down[None])


def solution(mesh):
    flat = P(AXES, None)
    deep = P(AXES, None, None)
    return jax.shard_map(
        on_device,
        mesh=mesh,
        in_specs=(flat, flat, flat, flat, deep, deep, deep),
        out_specs=(flat, flat, deep, deep, deep),
        check_vma=False,
    )
```

```python
import functools

import jax
import jax.numpy as jnp
from jax import lax
from jax.experimental import pallas as pl
from jax.experimental.pallas import tpu as pltpu
from jax.sharding import PartitionSpec as P

aux_weight = 1.0
CAP = 8
LANES = 128
ROWS = 256
AXES = ("dp", "expert")
f32 = jnp.float32
bf16 = jnp.bfloat16


def iota(shape, dim):
    return lax.broadcasted_iota(jnp.int32, shape, dim)


def nn(left, right):
    return jnp.dot(left, right, preferred_element_type=f32)


def nt(left, right):
    return lax.dot_general(left, right, (((1,), (1,)), ((), ())), preferred_element_type=f32)


def tn(left, right):
    return lax.dot_general(left, right, (((0,), (0,)), ((), ())), preferred_element_type=f32)


def in_hbm(array):
    return pltpu.with_memory_space_constraint(array, pltpu.HBM)


def in_vmem(array):
    return pltpu.with_memory_space_constraint(array, pltpu.VMEM)


def send_kernel(
    ids_hbm, probs_hbm, tok_hbm, grad_hbm, x_ref, pick_ref, w_ref, sum_ref, cnt_ref, ids_ref, probs_ref, tok_ref, grad_ref, sems
):
    toks, experts = probs_ref.shape
    slots, width = x_ref.shape[0], tok_ref.shape[1]
    pairs = ((ids_hbm, ids_ref), (probs_hbm, probs_ref), (tok_hbm, tok_ref), (grad_hbm, grad_ref))
    copies = [pltpu.make_async_copy(a, b, sems.at[i]) for i, (a, b) in enumerate(pairs)]
    for copy in copies:
        copy.start()

    copies[0].wait()
    expert = iota((experts, toks), 0)
    member_t = ids_ref[0:1, :] == expert
    for k in range(1, ids_ref.shape[0]):
        member_t = jnp.logical_or(member_t, ids_ref[k : k + 1, :] == expert)
    same = (iota((experts, experts), 0) == iota((experts, experts), 1)).astype(bf16)
    named = tn(member_t.astype(f32).astype(bf16), same)
    member = named > 0.5
    before = (iota((toks, toks), 0) > iota((toks, toks), 1)).astype(bf16)
    rank = nn(before, named.astype(bf16))
    rank = jnp.where(member, rank, 100.0).astype(bf16)
    copies[1].wait()
    picked = jnp.where(member, probs_ref[...], 0.0)
    total = jnp.sum(picked, axis=1, keepdims=True)
    weight = (picked / total).astype(bf16)

    w_ref[...] = weight.astype(f32)
    sum_ref[...] = jnp.broadcast_to(total, sum_ref.shape)
    count = jnp.sum(named, axis=0, keepdims=True)
    mine = iota(cnt_ref.shape, 0) % CAP == iota(cnt_ref.shape, 1) // (LANES // CAP)
    cnt_ref[...] = jnp.where(mine, jnp.broadcast_to(count, cnt_ref.shape), 0.0)
    spread_t = (iota((experts, slots), 0) == iota((experts, slots), 1) // CAP).astype(bf16)
    pick_ref[...] = (nn(rank, spread_t) == (iota((toks, slots), 1) % CAP).astype(f32)).astype(bf16)

    spread = (iota((slots, experts), 0) // CAP == iota((slots, experts), 1)).astype(bf16)
    chosen = nt(spread, rank) == (iota((slots, toks), 0) % CAP).astype(f32)
    weights = nt(spread, weight)
    weights = jnp.where(chosen, weights, 0.0).astype(bf16)
    chosen = chosen.astype(bf16)
    copies[2].wait()
    copies[3].wait()
    for at in range(0, width, 512):
        x_ref[:, at : at + 512] = nn(chosen, tok_ref[:, at : at + 512]).astype(bf16)
        x_ref[:, width + at : width + at + 512] = nn(weights, grad_ref[:, at : at + 512]).astype(bf16)


def send_rows(ids, probs, tokens, grads):
    toks, width = tokens.shape
    experts = probs.shape[1]
    slots = experts * CAP
    arrays = [in_hbm(a) for a in (ids.T, probs, tokens, grads)]
    return pl.pallas_call(
        send_kernel,
        in_specs=[pl.BlockSpec(memory_space=pltpu.HBM)] * 4,
        out_specs=[pl.BlockSpec(memory_space=pltpu.VMEM)] * 5,
        out_shape=[
            jax.ShapeDtypeStruct((slots, 2 * width), bf16),
            jax.ShapeDtypeStruct((toks, slots), bf16),
            jax.ShapeDtypeStruct((toks, experts), f32),
            jax.ShapeDtypeStruct((toks, experts), f32),
            jax.ShapeDtypeStruct((ROWS, LANES), f32),
        ],
        scratch_shapes=[pltpu.VMEM(a.shape, a.dtype) for a in arrays] + [pltpu.SemaphoreType.DMA((4,))],
        compiler_params=pltpu.CompilerParams(vmem_limit_bytes=24 << 20),
        name="send_rows",
    )(*arrays)


def expert_kernel(tok_ref, grad_ref, gate_ref, up_ref, down_ref, cnt_ref, out_ref, hid_ref, dg_ref, du_ref):
    rows, width = tok_ref.shape
    units = hid_ref.shape[1]
    terms = jnp.zeros((rows, LANES), f32)
    for at in range(0, units, 256):
        part = slice(at, at + 256)
        gate = nn(tok_ref[...], gate_ref[:, part])
        up = nn(tok_ref[...], up_ref[:, part])
        back = nt(grad_ref[...], down_ref[part, :])
        sig = jax.nn.sigmoid(gate)
        silu = gate * sig
        hidden = (silu * up).astype(bf16)
        hid_ref[:, part] = hidden
        term = hidden.astype(f32) * back
        terms += term[:, :LANES] + term[:, LANES:]
        dg_ref[:, part] = (back * up * sig * (1.0 + gate * (1.0 - sig))).astype(bf16)
        du_ref[:, part] = (back * silu).astype(bf16)
    d_gate = dg_ref[...]
    d_up = du_ref[...]
    for at in range(0, width, 512):
        cols = slice(at, at + 512)
        out_ref[:, cols] = (nt(d_gate, gate_ref[cols, :]) + nt(d_up, up_ref[cols, :])).astype(bf16)
    route = jnp.sum(terms, axis=1, keepdims=True)
    high = route.astype(bf16).astype(f32)
    turn = (iota((rows, LANES), 1) // (LANES // CAP) - iota((rows, LANES), 0) % CAP + CAP) % CAP
    extra = jnp.where(turn == 4, high, jnp.where(turn == 5, route - high, cnt_ref[...]))
    out_ref[:, width:] = extra.astype(bf16)


def expert_rows(x, gate, up, down, counts):
    slots = x.shape[0]
    width, units = gate.shape
    rows = counts.shape[0]
    whole = lambda shape: pl.BlockSpec(shape, lambda i: (0, 0), pipeline_mode=pl.Buffered(1))
    block = lambda cols, at: pl.BlockSpec((rows, cols), lambda i: (i, at))
    part = jax.ShapeDtypeStruct((slots, units), bf16)
    return pl.pallas_call(
        expert_kernel,
        grid=(slots // rows,),
        in_specs=[
            block(width, 0),
            block(width, 1),
            whole(gate.shape),
            whole(up.shape),
            whole(down.shape),
            whole(counts.shape),
        ],
        out_specs=[block(width + LANES, 0), block(units, 0), block(units, 0), block(units, 0)],
        out_shape=[jax.ShapeDtypeStruct((slots, width + LANES), bf16), part, part, part],
        compiler_params=pltpu.CompilerParams(vmem_limit_bytes=41 << 20),
        name="expert_rows",
    )(x, x, gate, up, down, counts)


def tail_kernel(scale, pick_ref, w_ref, sum_ref, back_hbm, tok_ref, prob_ref, extra_ref, back_ref, acc, sems):
    slots, width = back_ref.shape
    experts = w_ref.shape[1]
    blocks = [pl.ds(at, ROWS) for at in range(0, slots, ROWS)]
    first = pltpu.make_async_copy(back_hbm.at[:, pl.ds(width, LANES)], extra_ref, sems.at[len(blocks)])
    copies = [
        pltpu.make_async_copy(back_hbm.at[b, pl.ds(0, width)], back_ref.at[b], sems.at[i]) for i, b in enumerate(blocks)
    ]
    first.start()
    for copy in copies:
        copy.start()

    first.wait()
    row = iota((slots, LANES), 0)
    lane = iota((slots, LANES), 1)
    turn = (lane // (LANES // CAP) - row % CAP + CAP) % CAP
    extra = extra_ref[...].astype(f32)
    head = jnp.where(lane % (LANES // CAP) == 0, extra, 0.0)
    own = row // CAP == lane
    ones = jnp.ones((LANES, experts), bf16)
    high = nn(jnp.where(turn == 4, head, 0.0).astype(bf16), ones)
    low = nn(jnp.where(turn == 5, head, 0.0).astype(bf16), ones)
    route = nn(pick_ref[...], jnp.where(own, high, 0.0).astype(bf16))
    route += nn(pick_ref[...], jnp.where(own, low, 0.0).astype(bf16))
    load = jnp.sum(jnp.where(turn == 0, extra, 0.0), axis=0, keepdims=True)
    weight = w_ref[...]
    member = weight > 0.0
    route = jnp.where(member, route / jnp.where(member, weight, 1.0), 0.0)
    route = route.astype(bf16).astype(f32)
    mean = jnp.sum(route * weight, axis=1, keepdims=True)
    prob_ref[...] = jnp.where(member, (route - mean) / sum_ref[...], 0.0) + load * scale

    for i, block in enumerate(blocks):
        copies[i].wait()
        rows = nn(pick_ref[:, i * ROWS : (i + 1) * ROWS], back_ref[block, :])
        if i == 0:
            acc[...] = rows
        elif i < len(blocks) - 1:
            acc[...] += rows
        else:
            tok_ref[...] = (acc[...] + rows).astype(bf16)


def collect_rows(scale, pick, back, weight, total):
    toks, slots = pick.shape
    experts = weight.shape[1]
    width = back.shape[1] - LANES
    return pl.pallas_call(
        functools.partial(tail_kernel, scale),
        in_specs=[pl.BlockSpec(memory_space=pltpu.VMEM)] * 3 + [pl.BlockSpec(memory_space=pltpu.HBM)],
        out_specs=[pl.BlockSpec(memory_space=pltpu.VMEM)] * 2,
        out_shape=[jax.ShapeDtypeStruct((toks, width), bf16), jax.ShapeDtypeStruct((toks, experts), f32)],
        scratch_shapes=[
            pltpu.VMEM((slots, LANES), bf16),
            pltpu.VMEM((slots, width), bf16),
            pltpu.VMEM((toks, width), f32),
            pltpu.SemaphoreType.DMA((slots // ROWS + 1,)),
        ],
        compiler_params=pltpu.CompilerParams(vmem_limit_bytes=24 << 20),
        name="collect_rows",
    )(pick, weight, total, in_hbm(back))


def exchange(rows, devices):
    slots, width = rows.shape
    moved = lax.all_to_all(
        rows.reshape(devices, slots // devices, width), AXES, split_axis=0, concat_axis=0, tiled=True
    )
    return moved.reshape(slots, width)


def on_device(tokens, grad_out, probs, expert_ids, w_gate, w_up, w_down):
    toks, width = tokens.shape
    experts = probs.shape[1]
    devices = lax.axis_size("dp") * lax.axis_size("expert")
    x, pick, weight, total, counts = send_rows(expert_ids, probs, tokens, grad_out)
    x = exchange(x, devices)
    gate, up, down = [in_vmem(w[0]) for w in (w_gate, w_up, w_down)]
    out, hidden, d_gate_pre, d_up_pre = expert_rows(x, gate, up, down, counts)
    back = exchange(out, devices)
    d_gate = tn(x[:, :width], d_gate_pre).astype(bf16)
    d_up = tn(x[:, :width], d_up_pre).astype(bf16)
    d_down = tn(hidden, x[:, width:]).astype(bf16)
    scale = aux_weight * experts / (devices * toks * expert_ids.shape[1])
    d_tokens, d_probs = collect_rows(scale, pick, back, weight, total)
    return (d_tokens, d_probs, d_gate[None], d_up[None], d_down[None])


def solution(mesh):
    flat = P(AXES, None)
    deep = P(AXES, None, None)
    return jax.shard_map(
        on_device,
        mesh=mesh,
        in_specs=(flat, flat, flat, flat, deep, deep, deep),
        out_specs=(flat, flat, deep, deep, deep),
        check_vma=False,
    )
```

```python
import functools

import jax
import jax.numpy as jnp
from jax import lax
from jax.experimental import pallas as pl
from jax.experimental.pallas import tpu as pltpu
from jax.sharding import PartitionSpec as P

aux_weight = 1.0
CAP = 8
LANES = 128
ROWS = 256
AXES = ("dp", "expert")
f32 = jnp.float32
bf16 = jnp.bfloat16


def iota(shape, dim):
    return lax.broadcasted_iota(jnp.int32, shape, dim)


def nn(left, right):
    return jnp.dot(left, right, preferred_element_type=f32)


def nt(left, right):
    return lax.dot_general(left, right, (((1,), (1,)), ((), ())), preferred_element_type=f32)


def tn(left, right):
    return lax.dot_general(left, right, (((0,), (0,)), ((), ())), preferred_element_type=f32)


def in_hbm(array):
    return pltpu.with_memory_space_constraint(array, pltpu.HBM)


def in_vmem(array):
    return pltpu.with_memory_space_constraint(array, pltpu.VMEM)


def send_kernel(
    ids_hbm, probs_hbm, tok_hbm, grad_hbm, x_ref, pick_ref, w_ref, sum_ref, cnt_ref, ids_ref, probs_ref, tok_ref, grad_ref, sems
):
    toks, experts = probs_ref.shape
    slots, width = x_ref.shape[0], tok_ref.shape[1]
    pairs = ((ids_hbm, ids_ref), (probs_hbm, probs_ref), (tok_hbm, tok_ref), (grad_hbm, grad_ref))
    copies = [pltpu.make_async_copy(a, b, sems.at[i]) for i, (a, b) in enumerate(pairs)]
    for copy in copies:
        copy.start()

    copies[0].wait()
    expert = iota((experts, toks), 0)
    member_t = ids_ref[0:1, :] == expert
    for k in range(1, ids_ref.shape[0]):
        member_t = jnp.logical_or(member_t, ids_ref[k : k + 1, :] == expert)
    same = (iota((experts, experts), 0) == iota((experts, experts), 1)).astype(bf16)
    named = tn(member_t.astype(f32).astype(bf16), same)
    member = named > 0.5
    before = (iota((toks, toks), 0) > iota((toks, toks), 1)).astype(bf16)
    rank = nn(before, named.astype(bf16))
    rank = jnp.where(member, rank, 100.0).astype(bf16)
    copies[1].wait()
    picked = jnp.where(member, probs_ref[...], 0.0)
    total = jnp.sum(picked, axis=1, keepdims=True)
    weight = (picked / total).astype(bf16)

    w_ref[...] = weight.astype(f32)
    sum_ref[...] = jnp.broadcast_to(total, sum_ref.shape)
    count = jnp.sum(named, axis=0, keepdims=True)
    mine = iota(cnt_ref.shape, 0) % CAP == iota(cnt_ref.shape, 1) // (LANES // CAP)
    cnt_ref[...] = jnp.where(mine, jnp.broadcast_to(count, cnt_ref.shape), 0.0)
    spread_t = (iota((experts, slots), 0) == iota((experts, slots), 1) // CAP).astype(bf16)
    pick_ref[...] = (nn(rank, spread_t) == (iota((toks, slots), 1) % CAP).astype(f32)).astype(bf16)

    spread = (iota((slots, experts), 0) // CAP == iota((slots, experts), 1)).astype(bf16)
    chosen = nt(spread, rank) == (iota((slots, toks), 0) % CAP).astype(f32)
    weights = nt(spread, weight)
    weights = jnp.where(chosen, weights, 0.0).astype(bf16)
    chosen = chosen.astype(bf16)
    copies[2].wait()
    copies[3].wait()
    x_ref[:, :width] = nn(chosen, tok_ref[...]).astype(bf16)
    x_ref[:, width:] = nn(weights, grad_ref[...]).astype(bf16)


def send_rows(ids, probs, tokens, grads):
    toks, width = tokens.shape
    experts = probs.shape[1]
    slots = experts * CAP
    arrays = [in_hbm(a) for a in (ids.T, probs, tokens, grads)]
    return pl.pallas_call(
        send_kernel,
        in_specs=[pl.BlockSpec(memory_space=pltpu.HBM)] * 4,
        out_specs=[pl.BlockSpec(memory_space=pltpu.VMEM)] * 5,
        out_shape=[
            jax.ShapeDtypeStruct((slots, 2 * width), bf16),
            jax.ShapeDtypeStruct((toks, slots), bf16),
            jax.ShapeDtypeStruct((toks, experts), f32),
            jax.ShapeDtypeStruct((toks, experts), f32),
            jax.ShapeDtypeStruct((ROWS, LANES), f32),
        ],
        scratch_shapes=[pltpu.VMEM(a.shape, a.dtype) for a in arrays] + [pltpu.SemaphoreType.DMA((4,))],
        compiler_params=pltpu.CompilerParams(vmem_limit_bytes=24 << 20),
        name="send_rows",
    )(*arrays)


def expert_kernel(tok_ref, grad_ref, gate_ref, up_ref, down_ref, cnt_ref, out_ref, hid_ref, dg_ref, du_ref):
    rows, width = tok_ref.shape
    units = hid_ref.shape[1]
    terms = jnp.zeros((rows, LANES), f32)
    for at in range(0, units, 256):
        part = slice(at, at + 256)
        gate = nn(tok_ref[...], gate_ref[:, part])
        up = nn(tok_ref[...], up_ref[:, part])
        back = nt(grad_ref[...], down_ref[part, :])
        sig = jax.nn.sigmoid(gate)
        silu = gate * sig
        hidden = (silu * up).astype(bf16)
        hid_ref[:, part] = hidden
        term = hidden.astype(f32) * back
        terms += term[:, :LANES] + term[:, LANES:]
        dg_ref[:, part] = (back * up * sig * (1.0 + gate * (1.0 - sig))).astype(bf16)
        du_ref[:, part] = (back * silu).astype(bf16)
    route = jnp.sum(terms, axis=1, keepdims=True)
    high = route.astype(bf16).astype(f32)
    turn = (iota((rows, LANES), 1) // (LANES // CAP) - iota((rows, LANES), 0) % CAP + CAP) % CAP
    extra = jnp.where(turn == 4, high, jnp.where(turn == 5, route - high, cnt_ref[...]))
    out_ref[:, width:] = extra.astype(bf16)
    d_gate = dg_ref[...]
    d_up = du_ref[...]
    for at in range(0, width, 512):
        cols = slice(at, at + 512)
        out_ref[:, cols] = (nt(d_gate, gate_ref[cols, :]) + nt(d_up, up_ref[cols, :])).astype(bf16)


def expert_rows(x, gate, up, down, counts):
    slots = x.shape[0]
    width, units = gate.shape
    rows = counts.shape[0]
    whole = lambda shape: pl.BlockSpec(shape, lambda i: (0, 0), pipeline_mode=pl.Buffered(1))
    block = lambda cols, at: pl.BlockSpec((rows, cols), lambda i: (i, at))
    part = jax.ShapeDtypeStruct((slots, units), bf16)
    return pl.pallas_call(
        expert_kernel,
        grid=(slots // rows,),
        in_specs=[
            block(width, 0),
            block(width, 1),
            whole(gate.shape),
            whole(up.shape),
            whole(down.shape),
            whole(counts.shape),
        ],
        out_specs=[block(width + LANES, 0), block(units, 0), block(units, 0), block(units, 0)],
        out_shape=[jax.ShapeDtypeStruct((slots, width + LANES), bf16), part, part, part],
        compiler_params=pltpu.CompilerParams(vmem_limit_bytes=41 << 20),
        name="expert_rows",
    )(x, x, gate, up, down, counts)


def tail_kernel(scale, pick_ref, w_ref, sum_ref, back_hbm, tok_ref, prob_ref, extra_ref, back_ref, acc, sems):
    slots, width = back_ref.shape
    experts = w_ref.shape[1]
    blocks = [pl.ds(at, ROWS) for at in range(0, slots, ROWS)]
    first = pltpu.make_async_copy(back_hbm.at[:, pl.ds(width, LANES)], extra_ref, sems.at[len(blocks)])
    copies = [
        pltpu.make_async_copy(back_hbm.at[b, pl.ds(0, width)], back_ref.at[b], sems.at[i]) for i, b in enumerate(blocks)
    ]
    first.start()
    for copy in copies:
        copy.start()

    first.wait()
    row = iota((slots, LANES), 0)
    lane = iota((slots, LANES), 1)
    turn = (lane // (LANES // CAP) - row % CAP + CAP) % CAP
    extra = extra_ref[...].astype(f32)
    head = jnp.where(lane % (LANES // CAP) == 0, extra, 0.0)
    own = row // CAP == lane
    ones = jnp.ones((LANES, experts), bf16)
    high = nn(jnp.where(turn == 4, head, 0.0).astype(bf16), ones)
    low = nn(jnp.where(turn == 5, head, 0.0).astype(bf16), ones)
    route = nn(pick_ref[...], jnp.where(own, high, 0.0).astype(bf16))
    route += nn(pick_ref[...], jnp.where(own, low, 0.0).astype(bf16))
    load = jnp.sum(jnp.where(turn == 0, extra, 0.0), axis=0, keepdims=True)
    weight = w_ref[...]
    member = weight > 0.0
    route = jnp.where(member, route / jnp.where(member, weight, 1.0), 0.0)
    route = route.astype(bf16).astype(f32)
    mean = jnp.sum(route * weight, axis=1, keepdims=True)
    prob_ref[...] = jnp.where(member, (route - mean) / sum_ref[...], 0.0) + load * scale

    for i, block in enumerate(blocks):
        copies[i].wait()
        rows = nn(pick_ref[:, i * ROWS : (i + 1) * ROWS], back_ref[block, :])
        if i == 0:
            acc[...] = rows
        elif i < len(blocks) - 1:
            acc[...] += rows
        else:
            tok_ref[...] = (acc[...] + rows).astype(bf16)


def collect_rows(scale, pick, back, weight, total):
    toks, slots = pick.shape
    experts = weight.shape[1]
    width = back.shape[1] - LANES
    return pl.pallas_call(
        functools.partial(tail_kernel, scale),
        in_specs=[pl.BlockSpec(memory_space=pltpu.VMEM)] * 3 + [pl.BlockSpec(memory_space=pltpu.HBM)],
        out_specs=[pl.BlockSpec(memory_space=pltpu.VMEM)] * 2,
        out_shape=[jax.ShapeDtypeStruct((toks, width), bf16), jax.ShapeDtypeStruct((toks, experts), f32)],
        scratch_shapes=[
            pltpu.VMEM((slots, LANES), bf16),
            pltpu.VMEM((slots, width), bf16),
            pltpu.VMEM((toks, width), f32),
            pltpu.SemaphoreType.DMA((slots // ROWS + 1,)),
        ],
        compiler_params=pltpu.CompilerParams(vmem_limit_bytes=24 << 20),
        name="collect_rows",
    )(pick, weight, total, in_hbm(back))


def exchange(rows, devices):
    slots, width = rows.shape
    moved = lax.all_to_all(
        rows.reshape(devices, slots // devices, width), AXES, split_axis=0, concat_axis=0, tiled=True
    )
    return moved.reshape(slots, width)


def on_device(tokens, grad_out, probs, expert_ids, w_gate, w_up, w_down):
    toks, width = tokens.shape
    experts = probs.shape[1]
    devices = lax.axis_size("dp") * lax.axis_size("expert")
    x, pick, weight, total, counts = send_rows(expert_ids, probs, tokens, grad_out)
    x = exchange(x, devices)
    gate, up, down = [in_vmem(w[0]) for w in (w_gate, w_up, w_down)]
    out, hidden, d_gate_pre, d_up_pre = expert_rows(x, gate, up, down, counts)
    back = exchange(out, devices)
    d_gate = tn(x[:, :width], d_gate_pre).astype(bf16)
    d_up = tn(x[:, :width], d_up_pre).astype(bf16)
    d_down = tn(hidden, x[:, width:]).astype(bf16)
    scale = aux_weight * experts / (devices * toks * expert_ids.shape[1])
    d_tokens, d_probs = collect_rows(scale, pick, back, weight, total)
    return (d_tokens, d_probs, d_gate[None], d_up[None], d_down[None])


def solution(mesh):
    flat = P(AXES, None)
    deep = P(AXES, None, None)
    return jax.shard_map(
        on_device,
        mesh=mesh,
        in_specs=(flat, flat, flat, flat, deep, deep, deep),
        out_specs=(flat, flat, deep, deep, deep),
        check_vma=False,
    )
```
